32 devices in a mesh: section: 1, expert: 8 (over z, y), dp: 4 (over x, core).
Axes of the slice: x: 2, y: 2, z: 4, core: 2. Of those that a mesh axis runs over, the one named last changes fastest.
Arguments:
- fwd_resid: bfloat16 [1, 1024, 2048], P('section', 'expert', 'dp'), may hold values from -6 to 6
- fwd_normed: bfloat16 [1, 1024, 2048], P('section', 'expert', 'dp'), may hold values from -6 to 6
- fwd_routes: int32 [1, 1024, 8], P('section', 'expert'), may hold values from 0 to 15, all different within a row; in each aligned block of 128 rows (0 to 127, 128 to 255, ..., all dimensions but the last counted through in order) at most 65 rows name the same one
- fwd_probs: float32 [1, 1024, 8], P('section', 'expert'), may hold values from 0.02 to 0.3
- bwd_grad: bfloat16 [1, 1024, 2048], P('section', 'expert', 'dp'), may hold values from -6 to 6
- bwd_routes: int32 [1, 1024, 8], P('section', 'expert'), may hold values from 0 to 15, all different within a row; in each aligned block of 128 rows (0 to 127, 128 to 255, ..., all dimensions but the last counted through in order) at most 65 rows name the same one
- bwd_probs: float32 [1, 1024, 8], P('section', 'expert'), may hold values from 0.02 to 0.3
- saved_gate: bfloat16 [1, 32, 520, 192], P('section', ('expert', 'dp')), may hold values from -6 to 6
- saved_up: bfloat16 [1, 32, 520, 192], P('section', ('expert', 'dp')), may hold values from -6 to 6
- w_gate: bfloat16 [1, 32, 2048, 192], P('section', ('expert', 'dp')), may hold values from -0.125 to 0.125
- w_up: bfloat16 [1, 32, 2048, 192], P('section', ('expert', 'dp')), may hold values from -0.125 to 0.125
- w_down: bfloat16 [1, 32, 192, 2048], P('section', ('expert', 'dp')), may hold values from -0.3125 to 0.3125
Outputs:
- fwd_next: bfloat16 [1, 1024, 2048], P('section', 'expert', 'dp')
- bwd_next: bfloat16 [1, 1024, 2048], P('section', 'expert', 'dp')
The draws below stay inside these ranges and needn't reach their ends.
Inputs may be any that keep to these rules, and one draw needn't show every extreme that they name: `fwd_routes`: each token names 8 different experts. Within the tokens of one device (aligned blocks of 128 tokens of one section) no expert is named more than 65 times, a bound that some block reaches. `bwd_routes`: each token names 8 different experts. Within the tokens of one device (aligned blocks of 128 tokens of one section) no expert is named more than 65 times, a bound that some block reaches.
All inputs are finite; a program needn't handle non-finite values.
Results may differ from the reference program's by a relative error of at most 0.0065.
Values may be sent and summed in bfloat16 or wider, within the bound.
A program may use at most 64 MiB of HBM per device.

```python
import math
import jax
import jax.numpy as jnp
import numpy as np
from jax import lax

D = 2048
FF = 384
TOP = 8
TOK_DEV = 128
EXPERTS = 16
CAP = 65
TOKENS = 1024
SLOTS = 520
UNITS = 32
N_SECTION = 1
N_EXPERT = 8


def shard_levels(stream_key, extent, split, least, top_value):
    factor_of = 1.0
    for axis_at, parts in split:
        draws = jax.random.uniform(jax.random.fold_in(jax.random.fold_in(stream_key, 6), axis_at), (parts,), jnp.float32, least / len(split), top_value / len(split))
        factor_of = factor_of * jnp.repeat(jnp.exp(draws), extent[axis_at] // parts).reshape((-1,) + (1,) * (len(extent) - 1 - axis_at))
    return factor_of


def routed_block(own_key, own, number, rows, amount, top, most, skew):
    sequence = jax.random.permutation(own_key, amount)
    heavy_load, ordinary = shares(amount, rows * top, most, skew, True), shares(amount, rows * top, most, skew, False)
    places = jnp.arange(amount)

    def named(sizes, offset_by):
        used = int((sizes > 0).sum())
        fixed = max(1, used // 4)
        passed = fixed + (places - fixed + offset_by * (used - fixed)) % max(1, amount - fixed)
        return jnp.zeros((amount,), jnp.int32).at[sequence[jnp.where(places < fixed, places, passed)]].set(jnp.asarray(sizes, jnp.int32))

    sizes = jnp.where(number % 4 == 0, named(heavy_load, number // 4), named(ordinary, number - number // 4 - 1))
    mixed = jax.random.permutation(jax.random.fold_in(own, 3), amount)
    giver, sink = mixed[0:amount // 2 * 2:2], mixed[1:amount // 2 * 2:2]
    margin = jnp.minimum(sizes[giver] - 1, most - sizes[sink]) // 2
    margin = jnp.where((giver == sequence[0]) | (sink == sequence[0]) | (sizes[sink] == 0), 0, jnp.maximum(margin, 0))
    passed = jax.random.randint(jax.random.fold_in(own, 4), (amount // 2,), 0, 1 << 20) % (margin + 1)
    sizes = sizes.at[giver].add(-passed).at[sink].add(passed)
    labels = jnp.searchsorted(jnp.cumsum(sizes), jnp.arange(rows * top), side="right").astype(jnp.int32)
    grid = labels.reshape(top, rows).T
    grid = grid[jax.random.permutation(jax.random.fold_in(own, 1), rows)]
    offset_by = jax.random.randint(jax.random.fold_in(own, 2), (rows, 1), 0, top)
    return jnp.take_along_axis(grid, (jnp.arange(top)[None, :] + offset_by) % top, axis=1)


def shares(count, total, bound, slope, full):
    portions = [(1 << 20) // math.isqrt(standing ** slope) + 1 for standing in range(1, count + 1)]
    largest = bound if full else min(bound, max(-(-total // count), total * portions[0] // sum(portions)))
    least = 1 if total - largest >= count - 1 else 0
    counts, surplus = [largest] + [least] * (count - 1), total - largest - least * (count - 1)
    while surplus > 0:
        movable = [i for i in range(1, count) if counts[i] < largest] or [i for i in range(1, count) if counts[i] < bound]
        pool, left = sum([portions[i] for i in movable]), surplus
        for i in movable:
            addition = min(bound - counts[i], max(1, left * portions[i] // pool), surplus)
            counts[i] = counts[i] + addition
            surplus = surplus - addition
    return np.array(counts)


def normal_values(rng, extent, width, reach, cuts=(), held_as=jnp.bfloat16):
    values = width * jax.random.normal(rng, extent, jnp.float32)
    if cuts:
        values = values * shard_levels(rng, extent, cuts, -0.22, 0.18)
    return jnp.clip(values, -reach, reach).astype(held_as)


def setup_inputs(seed: int = 0) -> dict:
    streams_of = jax.random.split(jax.random.key(seed), 13)
    fwd_resid = normal_values(streams_of[0], (N_SECTION, TOKENS, D), 1.0, 6.0, ((1, 8), (2, 4)))
    fwd_normed = normal_values(streams_of[1], (N_SECTION, TOKENS, D), 1.0, 6.0, ((1, 8), (2, 4)))
    fwd_routes_keys = jax.random.split(jax.random.fold_in(streams_of[2], 1), N_SECTION * TOKENS // TOK_DEV)
    fwd_routes_turns = jax.random.permutation(jax.random.fold_in(streams_of[2], 3), N_SECTION * TOKENS // TOK_DEV)
    fwd_routes = jax.vmap(lambda own, number: routed_block(jax.random.fold_in(streams_of[2], 2), own, number, TOK_DEV, EXPERTS, TOP, CAP, 2))(fwd_routes_keys, fwd_routes_turns).reshape((N_SECTION, TOKENS, TOP))
    fwd_probs = jnp.clip(jnp.exp(math.log(0.3) - 2.7080503 * jax.random.uniform(streams_of[3], (N_SECTION, TOKENS, TOP), jnp.float32) ** shard_levels(streams_of[3], (N_SECTION, TOKENS, TOP), ((1, 8),), -0.2, 0.2)), 0.02, 0.3)
    bwd_grad = normal_values(streams_of[4], (N_SECTION, TOKENS, D), 1.0, 6.0, ((1, 8), (2, 4)))
    bwd_routes_keys = jax.random.split(jax.random.fold_in(streams_of[5], 1), N_SECTION * TOKENS // TOK_DEV)
    bwd_routes_turns = jax.random.permutation(jax.random.fold_in(streams_of[5], 3), N_SECTION * TOKENS // TOK_DEV)
    bwd_routes = jax.vmap(lambda own, number: routed_block(jax.random.fold_in(streams_of[5], 2), own, number, TOK_DEV, EXPERTS, TOP, CAP, 2))(bwd_routes_keys, bwd_routes_turns).reshape((N_SECTION, TOKENS, TOP))
    bwd_probs = jnp.clip(jnp.exp(math.log(0.3) - 2.7080503 * jax.random.uniform(streams_of[6], (N_SECTION, TOKENS, TOP), jnp.float32) ** shard_levels(streams_of[6], (N_SECTION, TOKENS, TOP), ((1, 8),), -0.2, 0.2)), 0.02, 0.3)
    saved_gate = normal_values(streams_of[7], (N_SECTION, UNITS, SLOTS, FF // 2), 1.0, 6.0, ((1, 32),))
    saved_up = normal_values(streams_of[8], (N_SECTION, UNITS, SLOTS, FF // 2), 1.0, 6.0, ((1, 32),))
    w_gate = normal_values(streams_of[9], (N_SECTION, UNITS, D, FF // 2), D ** -0.5, 0.125, ((1, 32),))
    w_up = normal_values(streams_of[10], (N_SECTION, UNITS, D, FF // 2), D ** -0.5, 0.125, ((1, 32),))
    w_down = normal_values(streams_of[11], (N_SECTION, UNITS, FF // 2, D), FF ** -0.5, 0.3125, ((1, 32),))
    return {"fwd_resid": fwd_resid, "fwd_normed": fwd_normed, "fwd_routes": fwd_routes, "fwd_probs": fwd_probs, "bwd_grad": bwd_grad, "bwd_routes": bwd_routes, "bwd_probs": bwd_probs, "saved_gate": saved_gate, "saved_up": saved_up, "w_gate": w_gate, "w_up": w_up, "w_down": w_down}


def slot_places(block_routes, experts):
    onehot = (block_routes[:, None] == jnp.arange(experts, dtype=jnp.int32)[None, :]).astype(jnp.int32)
    before = jnp.cumsum(onehot, axis=0) - onehot
    return jnp.sum(before * onehot, axis=1).astype(jnp.int32)


def slot_tables(routes_section):
    blocks = routes_section.reshape(N_EXPERT, TOK_DEV * TOP)
    places = jax.vmap(lambda block_rows: slot_places(block_rows, EXPERTS))(blocks)
    block_ids = jnp.arange(N_EXPERT, dtype=jnp.int32)[:, None] * CAP
    slot_ids = (places + block_ids).reshape(-1).astype(jnp.int32)
    flat_routes = routes_section.reshape(-1).astype(jnp.int32)
    token_ids = (jnp.arange(TOKENS * TOP, dtype=jnp.int32) // TOP).astype(jnp.int32)
    slot_table = jnp.full((EXPERTS, SLOTS), TOKENS, jnp.int32).at[flat_routes, slot_ids].set(token_ids)
    return slot_table, flat_routes, slot_ids


def mix_back(expert_rows, flat_routes, slot_ids, probs_section):
    gathered = expert_rows[flat_routes, slot_ids].astype(jnp.float32).reshape(TOKENS, TOP, D)
    return jnp.sum(probs_section[:, :, None].astype(jnp.float32) * gathered, axis=1)


def reference(fwd_resid, fwd_normed, fwd_routes, fwd_probs, bwd_grad, bwd_routes, bwd_probs, saved_gate, saved_up, w_gate, w_up, w_down):
    half_width = FF // 2
    fwd_layers = []
    bwd_layers = []
    for section_index in range(N_SECTION):
        gate_pairs = w_gate[section_index].reshape(EXPERTS, 2, D, half_width)
        up_pairs = w_up[section_index].reshape(EXPERTS, 2, D, half_width)
        down_pairs = w_down[section_index].reshape(EXPERTS, 2, half_width, D)
        saved_gates = saved_gate[section_index].reshape(EXPERTS, 2, SLOTS, half_width)
        saved_ups = saved_up[section_index].reshape(EXPERTS, 2, SLOTS, half_width)

        padded = jnp.concatenate([fwd_normed[section_index], jnp.zeros((1, D), fwd_normed.dtype)], axis=0)
        fwd_table, fwd_flat, fwd_slots = slot_tables(fwd_routes[section_index])

        def forward_expert(inputs_pair):
            slot_table, gate_pair, up_pair, down_pair = inputs_pair
            slot_rows = padded[slot_table]
            total = jnp.zeros((SLOTS, D), jnp.float32)
            for half_index in range(2):
                gate_val = jnp.dot(slot_rows, gate_pair[half_index], preferred_element_type=jnp.float32)
                up_val = jnp.dot(slot_rows, up_pair[half_index], preferred_element_type=jnp.float32)
                hidden = (jax.nn.silu(gate_val) * up_val).astype(jnp.bfloat16)
                result = jnp.dot(hidden, down_pair[half_index], preferred_element_type=jnp.float32).astype(jnp.bfloat16)
                total = total + result.astype(jnp.float32)
            return total.astype(jnp.bfloat16)

        fwd_expert = lax.map(forward_expert, (fwd_table, gate_pairs, up_pairs, down_pairs))
        mix_sum = mix_back(fwd_expert, fwd_flat, fwd_slots, fwd_probs[section_index])
        fwd_layers.append((fwd_resid[section_index].astype(jnp.float32) + mix_sum).astype(jnp.bfloat16))

        grad_padded = jnp.concatenate([bwd_grad[section_index], jnp.zeros((1, D), bwd_grad.dtype)], axis=0)
        bwd_table, bwd_flat, bwd_slots = slot_tables(bwd_routes[section_index])

        def backward_expert(inputs_pair):
            slot_table, gate_pair, up_pair, down_pair, gate_saved, up_saved = inputs_pair
            slot_rows = grad_padded[slot_table]
            total = jnp.zeros((SLOTS, D), jnp.float32)
            for half_index in range(2):
                grad_hidden = lax.dot_general(slot_rows, down_pair[half_index], (((1,), (1,)), ((), ())), preferred_element_type=jnp.float32)
                gate_val = gate_saved[half_index].astype(jnp.float32)
                up_val = up_saved[half_index].astype(jnp.float32)
                sig_gate = jax.nn.sigmoid(gate_val)
                grad_gate = (grad_hidden * up_val * sig_gate * (1.0 + gate_val * (1.0 - sig_gate))).astype(jnp.bfloat16)
                grad_up = (grad_hidden * jax.nn.silu(gate_val)).astype(jnp.bfloat16)
                result = lax.dot_general(grad_gate, gate_pair[half_index], (((1,), (1,)), ((), ())), preferred_element_type=jnp.float32)
                result = result + lax.dot_general(grad_up, up_pair[half_index], (((1,), (1,)), ((), ())), preferred_element_type=jnp.float32)
                total = total + result.astype(jnp.bfloat16).astype(jnp.float32)
            return total.astype(jnp.bfloat16)

        bwd_expert = lax.map(backward_expert, (bwd_table, gate_pairs, up_pairs, down_pairs, saved_gates, saved_ups))
        grad_sum = mix_back(bwd_expert, bwd_flat, bwd_slots, bwd_probs[section_index])
        bwd_layers.append(grad_sum.astype(jnp.bfloat16))
    fwd_layer = jnp.stack(fwd_layers, axis=0)
    bwd_layer = jnp.stack(bwd_layers, axis=0)
    return jnp.roll(fwd_layer, 1, axis=0), jnp.roll(bwd_layer, -1, axis=0)
```

```python
import functools

import jax
import jax.numpy as jnp
from jax import lax
from jax.experimental import pallas as pl
from jax.experimental.pallas import tpu as pltpu
from jax.sharding import PartitionSpec as P

F32 = jnp.float32
BF16 = jnp.bfloat16
MESH = pl.DeviceIdType.MESH


def round_up(value, unit):
    return -(-value // unit) * unit


def kernel(
    n, xs, top, cap,
    resid, normed, grad, rp, sg_hbm, su_hbm, wg_hbm, wu_hbm, wd_hbm,
    fwd_out, bwd_out,
    sg, su, wg, wu, wd, fac,
    meta_s, meta_z, meta_y, tok, rows, stag, keep, half_s, half_r, mixin, eo_s,
    yout, yin, zacc, zout, zin,
    load_sem, ms_sem, mr_sem, my_sem, zs_sem, zr_sem, ys_sem, yr_sem,
    xs_sem, xr_sem, cs_sem, cr_sem, hs_sem, hr_sem, es_sem, er_sem,
    ry_sem, rzs_sem, rzr_sem,
):
    half = n // 2
    tokens, width = normed.shape
    experts = n * xs
    chunk = rows.shape[-2]
    slots = sg_hbm.shape[0]
    e = lax.axis_index("expert")
    d = lax.axis_index("dp")
    hi, lo = lax.div(e, 2), lax.rem(e, 2)
    x, core = lax.div(d, 2), lax.rem(d, 2)

    def z_dev(k):
        return {"expert": lax.rem(hi + k, half) * 2 + lo, "dp": d}

    y_dev = {"expert": hi * 2 + 1 - lo, "dp": d}

    def x_dev(k):
        return {"expert": e, "dp": lax.rem(x + k, xs) * 2 + core}

    c_dev = {"expert": e, "dp": x * 2 + 1 - core}
    pending = []

    def send(src, dst, s_sem, r_sem, dev):
        copy = pltpu.make_async_remote_copy(
            src_ref=src, dst_ref=dst, send_sem=s_sem, recv_sem=r_sem,
            device_id=dev, device_id_type=MESH,
        )
        copy.start()
        pending.append(copy)

    def arrived(dst, s_sem, r_sem, dev):
        pltpu.make_async_remote_copy(
            src_ref=dst, dst_ref=dst, send_sem=s_sem, recv_sem=r_sem,
            device_id=dev, device_id_type=MESH,
        ).wait_recv()

    barrier = pltpu.get_barrier_semaphore()
    partners = [z_dev(k) for k in range(1, half)] + [y_dev]
    partners += [x_dev(k) for k in range(1, xs)] + [c_dev]
    for dev in partners:
        pl.semaphore_signal(barrier, inc=1, device_id=dev, device_id_type=MESH)

    loads = [
        pltpu.make_async_copy(a, b, load_sem.at[i])
        for i, (a, b) in enumerate(
            ((sg_hbm, sg), (su_hbm, su), (wg_hbm, wg), (wu_hbm, wu), (wd_hbm, wd))
        )
    ]
    for load in loads:
        load.start()

    expert_ids = lax.broadcasted_iota(jnp.int32, (experts, tokens), 0).astype(F32)
    tri = (
        lax.broadcasted_iota(jnp.int32, (tokens, tokens), 0)
        < lax.broadcasted_iota(jnp.int32, (tokens, tokens), 1)
    ).astype(F32).astype(BF16)
    for p in range(2):
        hits = jnp.zeros((experts, tokens), F32)
        weight = jnp.zeros((experts, tokens), F32)
        for j in range(top):
            same = rp[2 * p * top + j : 2 * p * top + j + 1, :] == expert_ids
            hits = hits + jnp.where(same, 1.0, 0.0)
            prob = rp[(2 * p + 1) * top + j : (2 * p + 1) * top + j + 1, :]
            weight = weight + jnp.where(same, prob, 0.0)
        before = jnp.dot(hits.astype(BF16), tri, preferred_element_type=F32)
        place = jnp.where(hits > 0.0, before, -1000000.0)
        for g in range(n):
            meta_s[g, 2 * p * xs : (2 * p + 1) * xs, :] = place[g * xs : (g + 1) * xs, :]
            meta_s[g, (2 * p + 1) * xs : (2 * p + 2) * xs, :] = weight[g * xs : (g + 1) * xs, :]
    meta_z[0, 0] = meta_s[e]
    meta_z[1, 0] = meta_s[hi * 2 + 1 - lo]

    pl.semaphore_wait(barrier, len(partners))

    for k in range(1, half):
        to = lax.rem(hi + k, half) * 2
        for c in range(2):
            send(
                meta_s.at[to + (lo if c == 0 else 1 - lo)], meta_z.at[c, half - k],
                ms_sem.at[c, k], mr_sem.at[c, half - k], z_dev(k),
            )
    sources = (normed, grad)
    for p in range(2):
        for k in range(1, half):
            send(sources[p], tok.at[p, 0, half - k], zs_sem.at[p, k], zr_sem.at[p, half - k], z_dev(k))
        send(sources[p], tok.at[p, 1, 0], ys_sem.at[p, 0], yr_sem.at[p, 0], y_dev)
        tok[p, 0, 0] = sources[p][...]

    def forward_y(p):
        for r in range(1, half):
            arrived(tok.at[p, 0, r], zs_sem.at[p, r], zr_sem.at[p, r], z_dev(r))
            send(tok.at[p, 0, r], tok.at[p, 1, r], ys_sem.at[p, r], yr_sem.at[p, r], y_dev)

    def meta_row(c, r, row):
        if c == 0:
            return meta_z[0, r, pl.ds(row, 1), :]
        return meta_y[r, pl.ds(row, 1), :]

    def pack(p, c):
        if c == 1:
            for r in range(half):
                arrived(tok.at[p, 1, r], ys_sem.at[p, r], yr_sem.at[p, r], y_dev)
        slot_ids = lax.broadcasted_iota(jnp.int32, (chunk, tokens), 0).astype(F32)
        block = tok[p, c].reshape(half * tokens, width)
        for k in list(range(1, xs)) + [0]:
            line = 2 * p * xs + lax.rem(x + k, xs)
            parts = [
                jnp.where(slot_ids == meta_row(c, r, line) + float(r * cap), 1.0, 0.0).astype(BF16)
                for r in range(half)
            ]
            packed = jnp.dot(
                jnp.concatenate(parts, axis=1), block, preferred_element_type=F32
            ).astype(BF16)
            if k == 0:
                rows[p, c, 0, 0] = packed
                send(rows.at[p, c, 0, 0], rows.at[p, c, 0, 1], cs_sem.at[p, c, 0], cr_sem.at[p, c, 0], c_dev)
            else:
                stag[p, c, k] = packed
                send(stag.at[p, c, k], rows.at[p, c, xs - k, 0], xs_sem.at[p, c, k], xr_sem.at[p, c, xs - k], x_dev(k))

    def forward_core(p, c):
        for r in range(1, xs):
            arrived(rows.at[p, c, r, 0], xs_sem.at[p, c, r], xr_sem.at[p, c, r], x_dev(r))
            send(rows.at[p, c, r, 0], rows.at[p, c, r, 1], cs_sem.at[p, c, r], cr_sem.at[p, c, r], c_dev)

    def feature(r, other):
        at = lax.rem(x + r, xs) * 2 + (1 - core if other else core)
        return pl.ds(pl.multiple_of(at * width, width), width)

    nt = (((1,), (1,)), ((), ()))

    def compute(p, c):
        parts = [(r, o) for r in range(xs) for o in range(2)]
        first, second = None, None
        for r, o in parts:
            if o == 1:
                arrived(rows.at[p, c, r, 1], cs_sem.at[p, c, r], cr_sem.at[p, c, r], c_dev)
            piece = rows[p, c, r, o]
            if p == 0:
                a = jnp.dot(piece, wg[feature(r, o), :], preferred_element_type=F32)
                b = jnp.dot(piece, wu[feature(r, o), :], preferred_element_type=F32)
                first = a if first is None else first + a
                second = b if second is None else second + b
            else:
                a = lax.dot_general(piece, wd[:, feature(r, o)], nt, preferred_element_type=F32)
                first = a if first is None else first + a
        if p == 0:
            hidden = (jax.nn.silu(first) * second).astype(BF16)
        else:
            grad_gate = (first * fac[0, c]).astype(BF16)
            grad_up = (first * fac[1, c]).astype(BF16)
        for o in (1, 0):
            for r in range(xs):
                if p == 0:
                    res = jnp.dot(hidden, wd[:, feature(r, o)], preferred_element_type=F32)
                else:
                    res = lax.dot_general(grad_gate, wg[feature(r, o), :], nt, preferred_element_type=F32)
                    res = res + lax.dot_general(grad_up, wu[feature(r, o), :], nt, preferred_element_type=F32)
                if o == 1:
                    half_s[p, c, r] = res.astype(BF16)
                    send(half_s.at[p, c, r], half_r.at[p, c, r], hs_sem.at[p, c, r], hr_sem.at[p, c, r], c_dev)
                else:
                    keep[p, c, r] = res.astype(BF16)

    def join(p, c):
        for r in list(range(1, xs)) + [0]:
            arrived(half_r.at[p, c, r], hs_sem.at[p, c, r], hr_sem.at[p, c, r], c_dev)
            total = (keep[p, c, r].astype(F32) + half_r[p, c, r].astype(F32)).astype(BF16)
            if r == 0:
                mixin[p, c, 0] = total
            else:
                eo_s[p, c, r] = total
                send(eo_s.at[p, c, r], mixin.at[p, c, xs - r], es_sem.at[p, c, r], er_sem.at[p, c, xs - r], x_dev(r))

    def mix(p, c):
        for r in range(1, xs):
            arrived(mixin.at[p, c, r], es_sem.at[p, c, r], er_sem.at[p, c, r], x_dev(r))
        slot_ids = lax.broadcasted_iota(jnp.int32, (tokens, chunk), 1).astype(F32)
        pad = round_up(2 * xs, 8) - 2 * xs
        for r in range(half):
            lines = []
            for k in range(xs):
                at = lax.rem(x + k, xs)
                lines.append(meta_row(c, r, 2 * p * xs + at))
                lines.append(meta_row(c, r, (2 * p + 1) * xs + at))
            if pad:
                lines.append(jnp.zeros((pad, tokens), F32))
            cols = jnp.concatenate(lines, axis=0).T
            mats = [
                jnp.where(
                    slot_ids == cols[:, 2 * k : 2 * k + 1] + float(r * cap),
                    cols[:, 2 * k + 1 : 2 * k + 2], 0.0,
                ).astype(BF16)
                for k in range(xs)
            ]
            out = jnp.zeros((tokens, width), F32)
            for k in range(xs):
                out = out + jnp.dot(mats[k], mixin[p, c, k], preferred_element_type=F32)
            if c == 1:
                yout[p, r] = out.astype(BF16)
                send(yout.at[p, r], yin.at[p, r], ry_sem.at[0, p, r], ry_sem.at[1, p, r], y_dev)
            else:
                zacc[p, r] = out

    def scatter_z(p):
        for r in list(range(1, half)) + [0]:
            arrived(yin.at[p, r], ry_sem.at[0, p, r], ry_sem.at[1, p, r], y_dev)
            total = zacc[p, r] + yin[p, r].astype(F32)
            if r == 0:
                zacc[p, 0] = total
            else:
                zout[p, r] = total.astype(BF16)
                send(zout.at[p, r], zin.at[p, half - r], rzs_sem.at[p, r], rzr_sem.at[p, half - r], z_dev(r))

    def finish(p):
        total = zacc[p, 0]
        if p == 0:
            total = total + resid[...].astype(F32)
        for r in range(1, half):
            arrived(zin.at[p, r], rzs_sem.at[p, r], rzr_sem.at[p, r], z_dev(r))
            total = total + zin[p, r].astype(F32)
        (fwd_out, bwd_out)[p][...] = total.astype(BF16)

    loads[0].wait()
    loads[1].wait()
    for c in range(2):
        at = lax.broadcasted_iota(jnp.int32, (chunk, slots), 0)
        turn = jnp.zeros((chunk, slots), jnp.int32)
        for k in range(1, half):
            turn = turn + jnp.where(at >= k * cap, 1, 0)
        place = at - turn * cap
        turn = turn + hi
        turn = jnp.where(turn >= half, turn - half, turn)
        origin = (turn * 2 + (lo if c == 0 else 1 - lo)) * cap + place
        hit = (origin == lax.broadcasted_iota(jnp.int32, (chunk, slots), 1)) & (at < half * cap)
        perm = jnp.where(hit, 1.0, 0.0).astype(BF16)
        gval = jnp.dot(perm, sg[...], preferred_element_type=F32)
        uval = jnp.dot(perm, su[...], preferred_element_type=F32)
        sig = jax.nn.sigmoid(gval)
        fac[0, c] = uval * sig * (1.0 + gval * (1.0 - sig))
        fac[1, c] = gval * sig

    for k in range(1, half):
        for c in range(2):
            arrived(meta_z.at[c, k], ms_sem.at[c, k], mr_sem.at[c, k], z_dev(k))
    send(meta_z.at[1], meta_y, my_sem.at[0], my_sem.at[1], y_dev)
    forward_y(0)
    pack(0, 0)
    forward_y(1)
    arrived(meta_y, my_sem.at[0], my_sem.at[1], y_dev)
    pack(0, 1)
    forward_core(0, 0)
    pack(1, 0)
    forward_core(0, 1)
    for load in loads[2:]:
        load.wait()
    compute(0, 1)
    pack(1, 1)
    join(0, 1)
    compute(0, 0)
    forward_core(1, 0)
    join(0, 0)
    forward_core(1, 1)
    mix(0, 1)
    compute(1, 1)
    join(1, 1)
    mix(0, 0)
    scatter_z(0)
    compute(1, 0)
    join(1, 0)
    mix(1, 1)
    mix(1, 0)
    finish(0)
    scatter_z(1)
    finish(1)
    for copy in pending:
        copy.wait_send()


def body(
    fwd_resid, fwd_normed, fwd_routes, fwd_probs, bwd_grad, bwd_routes, bwd_probs,
    saved_gate, saved_up, w_gate, w_up, w_down,
):
    n = lax.axis_size("expert")
    dp = lax.axis_size("dp")
    sections = lax.axis_size("section")
    xs = dp // 2
    half = n // 2
    tokens, width = fwd_normed.shape[1:]
    top = fwd_routes.shape[2]
    slots, hidden = saved_gate.shape[2:]
    feats = w_gate.shape[2]
    cap = slots // n
    chunk = round_up(half * cap, 16)
    meta_rows = 4 * xs
    rp = jnp.concatenate(
        [
            fwd_routes[0].astype(F32).T, fwd_probs[0].T,
            bwd_routes[0].astype(F32).T, bwd_probs[0].T,
        ],
        axis=0,
    )
    vmem = pl.BlockSpec(memory_space=pltpu.VMEM)
    hbm = pl.BlockSpec(memory_space=pl.ANY)
    dma = pltpu.SemaphoreType.DMA
    out = jax.ShapeDtypeStruct((tokens, width), BF16)
    fwd_out, bwd_out = pl.pallas_call(
        functools.partial(kernel, n, xs, top, cap),
        out_shape=(out, out),
        in_specs=[vmem] * 4 + [hbm] * 5,
        out_specs=(vmem, vmem),
        scratch_shapes=[
            pltpu.VMEM((slots, hidden), BF16),
            pltpu.VMEM((slots, hidden), BF16),
            pltpu.VMEM((feats, hidden), BF16),
            pltpu.VMEM((feats, hidden), BF16),
            pltpu.VMEM((hidden, feats), BF16),
            pltpu.VMEM((2, 2, chunk, hidden), F32),
            pltpu.VMEM((n, meta_rows, tokens), F32),
            pltpu.VMEM((2, half, meta_rows, tokens), F32),
            pltpu.VMEM((half, meta_rows, tokens), F32),
            pltpu.VMEM((2, 2, half, tokens, width), BF16),
            pltpu.VMEM((2, 2, xs, 2, chunk, width), BF16),
            pltpu.VMEM((2, 2, xs, chunk, width), BF16),
            pltpu.VMEM((2, 2, xs, chunk, width), BF16),
            pltpu.VMEM((2, 2, xs, chunk, width), BF16),
            pltpu.VMEM((2, 2, xs, chunk, width), BF16),
            pltpu.VMEM((2, 2, xs, chunk, width), BF16),
            pltpu.VMEM((2, 2, xs, chunk, width), BF16),
            pltpu.VMEM((2, half, tokens, width), BF16),
            pltpu.VMEM((2, half, tokens, width), BF16),
            pltpu.VMEM((2, half, tokens, width), F32),
            pltpu.VMEM((2, half, tokens, width), BF16),
            pltpu.VMEM((2, half, tokens, width), BF16),
            dma((5,)),
            dma((2, half)), dma((2, half)), dma((2,)),
            dma((2, half)), dma((2, half)), dma((2, half)), dma((2, half)),
            dma((2, 2, xs)), dma((2, 2, xs)), dma((2, 2, xs)), dma((2, 2, xs)),
            dma((2, 2, xs)), dma((2, 2, xs)), dma((2, 2, xs)), dma((2, 2, xs)),
            dma((2, 2, half)), dma((2, half)), dma((2, half)),
        ],
        compiler_params=pltpu.CompilerParams(
            collective_id=0, has_side_effects=True, vmem_limit_bytes=60 * 1024 * 1024
        ),
    )(
        fwd_resid[0], fwd_normed[0], bwd_grad[0], rp,
        saved_gate[0, 0], saved_up[0, 0], w_gate[0, 0], w_up[0, 0], w_down[0, 0],
    )
    fwd_next, bwd_next = fwd_out[None], bwd_out[None]
    if sections > 1:
        up = [(i, (i + 1) % sections) for i in range(sections)]
        fwd_next = lax.ppermute(fwd_next, "section", up)
        bwd_next = lax.ppermute(bwd_next, "section", [(j, i) for i, j in up])
    return (fwd_next, bwd_next)


def solution(mesh):
    tok = P("section", "expert", "dp")
    route = P("section", "expert", None)
    unit = P("section", ("expert", "dp"), None, None)
    return jax.shard_map(
        body,
        mesh=mesh,
        in_specs=(tok, tok, route, route, tok, route, route, unit, unit, unit, unit, unit),
        out_specs=(tok, tok),
        check_vma=False,
    )
```

```python
import functools

import jax
import jax.numpy as jnp
from jax import lax
from jax.experimental import pallas as pl
from jax.experimental.pallas import tpu as pltpu
from jax.sharding import PartitionSpec as P

F32 = jnp.float32
BF16 = jnp.bfloat16
MESH = pl.DeviceIdType.MESH


def round_up(value, unit):
    return -(-value // unit) * unit


def kernel(
    n, xs, top, cap,
    normed, grad, fr, fp, br, bp, sg_hbm, su_hbm, wg_hbm, wu_hbm, wd_hbm,
    fwd_out, bwd_out,
    sg, su, wg, wu, wd, fac,
    meta_s, meta_z, meta_y, tok, rows, stag, keep, half_s, half_r, mixin, eo_s,
    yout, yin, zacc, zout, zin,
    load_sem, ms_sem, mr_sem, my_sem, zs_sem, zr_sem, ys_sem, yr_sem,
    xs_sem, xr_sem, cs_sem, cr_sem, hs_sem, hr_sem, es_sem, er_sem,
    ry_sem, rzs_sem, rzr_sem,
):
    half = n // 2
    tokens, width = normed.shape
    experts = n * xs
    chunk = rows.shape[-2]
    slots = sg_hbm.shape[1]
    e = lax.axis_index("expert")
    d = lax.axis_index("dp")
    hi, lo = lax.div(e, 2), lax.rem(e, 2)
    x, core = lax.div(d, 2), lax.rem(d, 2)

    def z_dev(k):
        return {"expert": lax.rem(hi + k, half) * 2 + lo, "dp": d}

    y_dev = {"expert": hi * 2 + 1 - lo, "dp": d}

    def x_dev(k):
        return {"expert": e, "dp": lax.rem(x + k, xs) * 2 + core}

    c_dev = {"expert": e, "dp": x * 2 + 1 - core}
    pending = []

    def send(src, dst, s_sem, r_sem, dev):
        copy = pltpu.make_async_remote_copy(
            src_ref=src, dst_ref=dst, send_sem=s_sem, recv_sem=r_sem,
            device_id=dev, device_id_type=MESH,
        )
        copy.start()
        pending.append(copy)

    def arrived(dst, s_sem, r_sem, dev):
        pltpu.make_async_remote_copy(
            src_ref=dst, dst_ref=dst, send_sem=s_sem, recv_sem=r_sem,
            device_id=dev, device_id_type=MESH,
        ).wait_recv()

    barrier = pltpu.get_barrier_semaphore()
    partners = [z_dev(k) for k in range(1, half)] + [y_dev]
    partners += [x_dev(k) for k in range(1, xs)] + [c_dev]
    for dev in partners:
        pl.semaphore_signal(barrier, inc=1, device_id=dev, device_id_type=MESH)

    loads = [
        pltpu.make_async_copy(a, b, load_sem.at[i])
        for i, (a, b) in enumerate(
            ((sg_hbm, sg), (su_hbm, su), (wg_hbm, wg), (wu_hbm, wu), (wd_hbm, wd))
        )
    ]
    for load in loads:
        load.start()

    expert_ids = lax.broadcasted_iota(jnp.int32, (experts, tokens), 0)
    tri = (
        lax.broadcasted_iota(jnp.int32, (tokens, tokens), 0)
        < lax.broadcasted_iota(jnp.int32, (tokens, tokens), 1)
    ).astype(F32).astype(BF16)
    for p, (routes, probs) in enumerate(((fr, fp), (br, bp))):
        hits = jnp.zeros((experts, tokens), F32)
        weight = jnp.zeros((experts, tokens), F32)
        for j in range(top):
            same = routes[j : j + 1, :] == expert_ids
            hits = hits + jnp.where(same, 1.0, 0.0)
            weight = weight + jnp.where(same, probs[j : j + 1, :], 0.0)
        before = jnp.dot(hits.astype(BF16), tri, preferred_element_type=F32)
        place = jnp.where(hits > 0.0, before, -1000000.0)
        for g in range(n):
            meta_s[g, 2 * p * xs : (2 * p + 1) * xs, :] = place[g * xs : (g + 1) * xs, :]
            meta_s[g, (2 * p + 1) * xs : (2 * p + 2) * xs, :] = weight[g * xs : (g + 1) * xs, :]
    meta_z[0, 0] = meta_s[e]
    sources = (normed, grad)
    for p in range(2):
        tok[p, 0, 0] = sources[p][...]

    pl.semaphore_wait(barrier, len(partners))

    send(meta_s.at[hi * 2 + 1 - lo], meta_y.at[0], my_sem.at[0, 0], my_sem.at[1, 0], y_dev)
    for k in range(1, half):
        to = lax.rem(hi + k, half) * 2
        for c in range(2):
            send(
                meta_s.at[to + (lo if c == 0 else 1 - lo)], meta_z.at[c, half - k],
                ms_sem.at[c, k], mr_sem.at[c, half - k], z_dev(k),
            )

    def start_y(p):
        send(sources[p], tok.at[p, 0, 1], ys_sem.at[p, 0], yr_sem.at[p, 0], y_dev)

    start_y(0)
    for p in range(2):
        for k in range(1, half):
            send(sources[p], tok.at[p, half - k, 0], zs_sem.at[p, k], zr_sem.at[p, half - k], z_dev(k))

    def forward_y(p, r):
        if r == 0:
            if p == 1:
                start_y(1)
            return
        if p == 0:
            for c in range(2):
                arrived(meta_z.at[c, r], ms_sem.at[c, r], mr_sem.at[c, r], z_dev(r))
            send(meta_z.at[1, r], meta_y.at[r], my_sem.at[0, r], my_sem.at[1, r], y_dev)
        arrived(tok.at[p, r, 0], zs_sem.at[p, r], zr_sem.at[p, r], z_dev(r))
        send(tok.at[p, r, 0], tok.at[p, r, 1], ys_sem.at[p, r], yr_sem.at[p, r], y_dev)

    def meta_row(c, r, row):
        if c == 0:
            return meta_z[0, r, pl.ds(row, 1), :]
        return meta_y[r, pl.ds(row, 1), :]

    def pack(p, r):
        if p == 0:
            arrived(meta_y.at[r], my_sem.at[0, r], my_sem.at[1, r], y_dev)
        arrived(tok.at[p, r, 1], ys_sem.at[p, r], yr_sem.at[p, r], y_dev)
        slot_ids = lax.broadcasted_iota(jnp.int32, (chunk, tokens), 0).astype(F32)
        block = tok[p, r].reshape(2 * tokens, width)
        for k in list(range(1, xs)) + [0]:
            line = 2 * p * xs + lax.rem(x + k, xs)
            parts = [
                jnp.where(slot_ids == meta_row(c, r, line) + float(c * cap), 1.0, 0.0).astype(BF16)
                for c in range(2)
            ]
            packed = jnp.dot(
                jnp.concatenate(parts, axis=1), block, preferred_element_type=F32
            ).astype(BF16)
            if k == 0:
                rows[p, r, 0, 0] = packed
                send(rows.at[p, r, 0, 0], rows.at[p, r, 0, 1], cs_sem.at[p, r, 0], cr_sem.at[p, r, 0], c_dev)
            else:
                stag[p, r, k] = packed
                send(stag.at[p, r, k], rows.at[p, r, xs - k, 0], xs_sem.at[p, r, k], xr_sem.at[p, r, xs - k], x_dev(k))

    def forward_core(p, r):
        for k in range(1, xs):
            arrived(rows.at[p, r, k, 0], xs_sem.at[p, r, k], xr_sem.at[p, r, k], x_dev(k))
            send(rows.at[p, r, k, 0], rows.at[p, r, k, 1], cs_sem.at[p, r, k], cr_sem.at[p, r, k], c_dev)

    def feature(k, other):
        at = lax.rem(x + k, xs) * 2 + (1 - core if other else core)
        return pl.ds(pl.multiple_of(at * width, width), width)

    nt = (((1,), (1,)), ((), ()))

    def compute(p, r):
        first, second = None, None
        for k in range(xs):
            for o in range(2):
                if o == 1:
                    arrived(rows.at[p, r, k, 1], cs_sem.at[p, r, k], cr_sem.at[p, r, k], c_dev)
                piece = rows[p, r, k, o]
                if p == 0:
                    a = lax.dot_general(piece, wg[:, feature(k, o)], nt, preferred_element_type=F32)
                    b = lax.dot_general(piece, wu[:, feature(k, o)], nt, preferred_element_type=F32)
                    first = a if first is None else first + a
                    second = b if second is None else second + b
                else:
                    a = lax.dot_general(piece, wd[:, feature(k, o)], nt, preferred_element_type=F32)
                    first = a if first is None else first + a
        if p == 0:
            hidden = (jax.nn.silu(first) * second).astype(BF16)
        else:
            grad_gate = (first * fac[0, r]).astype(BF16)
            grad_up = (first * fac[1, r]).astype(BF16)
        for o in (1, 0):
            for k in range(xs):
                if p == 0:
                    res = jnp.dot(hidden, wd[:, feature(k, o)], preferred_element_type=F32)
                else:
                    res = jnp.dot(grad_gate, wg[:, feature(k, o)], preferred_element_type=F32)
                    res = res + jnp.dot(grad_up, wu[:, feature(k, o)], preferred_element_type=F32)
                if o == 1:
                    half_s[p, r, k] = res.astype(BF16)
                    send(half_s.at[p, r, k], half_r.at[p, r, k], hs_sem.at[p, r, k], hr_sem.at[p, r, k], c_dev)
                else:
                    keep[p, r, k] = res.astype(BF16)

    def join(p, r):
        for k in list(range(1, xs)) + [0]:
            arrived(half_r.at[p, r, k], hs_sem.at[p, r, k], hr_sem.at[p, r, k], c_dev)
            total = (keep[p, r, k].astype(F32) + half_r[p, r, k].astype(F32)).astype(BF16)
            if k == 0:
                mixin[p, r, 0] = total
            else:
                eo_s[p, r, k] = total
                send(eo_s.at[p, r, k], mixin.at[p, r, xs - k], es_sem.at[p, r, k], er_sem.at[p, r, xs - k], x_dev(k))

    def mix(p, r):
        for k in range(1, xs):
            arrived(mixin.at[p, r, k], es_sem.at[p, r, k], er_sem.at[p, r, k], x_dev(k))
        slot_ids = lax.broadcasted_iota(jnp.int32, (tokens, chunk), 1).astype(F32)
        pad = round_up(2 * xs, 8) - 2 * xs
        for c in (1, 0):
            lines = []
            for k in range(xs):
                at = lax.rem(x + k, xs)
                lines.append(meta_row(c, r, 2 * p * xs + at))
                lines.append(meta_row(c, r, (2 * p + 1) * xs + at))
            if pad:
                lines.append(jnp.zeros((pad, tokens), F32))
            cols = jnp.concatenate(lines, axis=0).T
            out = jnp.zeros((tokens, width), F32)
            for k in range(xs):
                mat = jnp.where(
                    slot_ids == cols[:, 2 * k : 2 * k + 1] + float(c * cap),
                    cols[:, 2 * k + 1 : 2 * k + 2], 0.0,
                ).astype(BF16)
                out = out + jnp.dot(mat, mixin[p, r, k], preferred_element_type=F32)
            if c == 1:
                yout[p, r] = out.astype(BF16)
                send(yout.at[p, r], yin.at[p, r], ry_sem.at[0, p, r], ry_sem.at[1, p, r], y_dev)
            else:
                zacc[p, r] = out

    def scatter_z(p, r):
        arrived(yin.at[p, r], ry_sem.at[0, p, r], ry_sem.at[1, p, r], y_dev)
        total = zacc[p, r] + yin[p, r].astype(F32)
        if r == 0:
            zacc[p, 0] = total
        else:
            zout[p, r] = total.astype(BF16)
            send(zout.at[p, r], zin.at[p, half - r], rzs_sem.at[p, r], rzr_sem.at[p, half - r], z_dev(r))

    def finish(p):
        total = zacc[p, 0]
        for r in range(1, half):
            arrived(zin.at[p, r], rzs_sem.at[p, r], rzr_sem.at[p, r], z_dev(r))
            total = total + zin[p, r].astype(F32)
        (fwd_out, bwd_out)[p][...] = total

    def factors(r):
        at = lax.broadcasted_iota(jnp.int32, (chunk, slots), 0)
        late = at >= cap
        turn = hi + r
        turn = jnp.where(turn >= half, turn - half, turn)
        origin = jnp.where(late, (turn * 2 + 1 - lo) * cap - cap, (turn * 2 + lo) * cap) + at
        hit = (origin == lax.broadcasted_iota(jnp.int32, (chunk, slots), 1)) & (at < 2 * cap)
        perm = jnp.where(hit, 1.0, 0.0).astype(BF16)
        gval = lax.dot_general(perm, sg[...], nt, preferred_element_type=F32)
        uval = lax.dot_general(perm, su[...], nt, preferred_element_type=F32)
        sig = jax.nn.sigmoid(gval)
        fac[0, r] = uval * sig * (1.0 + gval * (1.0 - sig))
        fac[1, r] = gval * sig

    back = list(range(half - 1, 0, -1))
    items = [(0, 0)] + [(0, r) for r in back] + [(1, r) for r in back] + [(1, 0)]
    count = len(items)
    stages = (
        (0, pack), (1, forward_core), (2, compute), (3, join), (4, mix), (5, scatter_z)
    )
    for load in loads[:2]:
        load.wait()
    for step in range(count + 5):
        if step + 1 < count:
            forward_y(*items[step + 1])
        if step == 2:
            for load in loads[2:]:
                load.wait()
        for lag, stage in stages:
            if 0 <= step - lag < count:
                stage(*items[step - lag])
        if step < half:
            factors(step)
    finish(0)
    finish(1)
    for copy in pending:
        copy.wait_send()


def body(
    fwd_resid, fwd_normed, fwd_routes, fwd_probs, bwd_grad, bwd_routes, bwd_probs,
    saved_gate, saved_up, w_gate, w_up, w_down,
):
    n = lax.axis_size("expert")
    dp = lax.axis_size("dp")
    sections = lax.axis_size("section")
    xs = dp // 2
    half = n // 2
    tokens, width = fwd_normed.shape[1:]
    top = fwd_routes.shape[2]
    slots, hidden = saved_gate.shape[2:]
    feats = w_gate.shape[2]
    cap = slots // n
    chunk = round_up(2 * cap, 8)
    meta_rows = 4 * xs
    vmem = pl.BlockSpec(memory_space=pltpu.VMEM)
    hbm = pl.BlockSpec(memory_space=pl.ANY)
    dma = pltpu.SemaphoreType.DMA
    out = jax.ShapeDtypeStruct((tokens, width), F32)
    fwd_sum, bwd_sum = pl.pallas_call(
        functools.partial(kernel, n, xs, top, cap),
        out_shape=(out, out),
        in_specs=[vmem] * 6 + [hbm] * 5,
        out_specs=(vmem, vmem),
        scratch_shapes=[
            pltpu.VMEM((hidden, slots), BF16),
            pltpu.VMEM((hidden, slots), BF16),
            pltpu.VMEM((hidden, feats), BF16),
            pltpu.VMEM((hidden, feats), BF16),
            pltpu.VMEM((hidden, feats), BF16),
            pltpu.VMEM((2, half, chunk, hidden), F32),
            pltpu.VMEM((n, meta_rows, tokens), F32),
            pltpu.VMEM((2, half, meta_rows, tokens), F32),
            pltpu.VMEM((half, meta_rows, tokens), F32),
            pltpu.VMEM((2, half, 2, tokens, width), BF16),
            pltpu.VMEM((2, half, xs, 2, chunk, width), BF16),
            pltpu.VMEM((2, half, xs, chunk, width), BF16),
            pltpu.VMEM((2, half, xs, chunk, width), BF16),
            pltpu.VMEM((2, half, xs, chunk, width), BF16),
            pltpu.VMEM((2, half, xs, chunk, width), BF16),
            pltpu.VMEM((2, half, xs, chunk, width), BF16),
            pltpu.VMEM((2, half, xs, chunk, width), BF16),
            pltpu.VMEM((2, half, tokens, width), BF16),
            pltpu.VMEM((2, half, tokens, width), BF16),
            pltpu.VMEM((2, half, tokens, width), F32),
            pltpu.VMEM((2, half, tokens, width), BF16),
            pltpu.VMEM((2, half, tokens, width), BF16),
            dma((5,)),
            dma((2, half)), dma((2, half)), dma((2, half)),
            dma((2, half)), dma((2, half)), dma((2, half)), dma((2, half)),
            dma((2, half, xs)), dma((2, half, xs)), dma((2, half, xs)), dma((2, half, xs)),
            dma((2, half, xs)), dma((2, half, xs)), dma((2, half, xs)), dma((2, half, xs)),
            dma((2, 2, half)), dma((2, half)), dma((2, half)),
        ],
        compiler_params=pltpu.CompilerParams(
            collective_id=0, has_side_effects=True, vmem_limit_bytes=60 * 1024 * 1024
        ),
    )(
        fwd_normed[0], bwd_grad[0],
        fwd_routes[0].T, fwd_probs[0].T, bwd_routes[0].T, bwd_probs[0].T,
        saved_gate[0, 0].T, saved_up[0, 0].T, w_gate[0, 0].T, w_up[0, 0].T, w_down[0, 0],
    )
    fwd_next = (fwd_resid.astype(F32) + fwd_sum[None]).astype(BF16)
    bwd_next = bwd_sum[None].astype(BF16)
    if sections > 1:
        up = [(i, (i + 1) % sections) for i in range(sections)]
        fwd_next = lax.ppermute(fwd_next, "section", up)
        bwd_next = lax.ppermute(bwd_next, "section", [(j, i) for i, j in up])
    return (fwd_next, bwd_next)


def solution(mesh):
    tok = P("section", "expert", "dp")
    route = P("section", "expert", None)
    unit = P("section", ("expert", "dp"), None, None)
    return jax.shard_map(
        body,
        mesh=mesh,
        in_specs=(tok, tok, route, route, tok, route, route, unit, unit, unit, unit, unit),
        out_specs=(tok, tok),
        check_vma=False,
    )
```

```python
import functools

import jax
import jax.numpy as jnp
from jax import lax
from jax.experimental import pallas as pl
from jax.experimental.pallas import tpu as pltpu
from jax.sharding import PartitionSpec as P

F32 = jnp.float32
BF16 = jnp.bfloat16
MESH = pl.DeviceIdType.MESH


def round_up(value, unit):
    return -(-value // unit) * unit


def kernel(
    n, xs, top, cap,
    normed, grad, fr, fp, br, bp, sg_hbm, su_hbm, wg_hbm, wu_hbm, wd_hbm,
    fwd_out, bwd_out,
    sg, su, wg, wu, wd, fac,
    meta_s, meta_z, meta_y, tok, rows, stag, keep, half_s, half_r, mixin, eo_s,
    yout, yin, zacc, zout, zin,
    load_sem, ms_sem, mr_sem, my_sem, zs_sem, zr_sem, ys_sem, yr_sem,
    xs_sem, xr_sem, cs_sem, cr_sem, hs_sem, hr_sem, es_sem, er_sem,
    ry_sem, rzs_sem, rzr_sem,
):
    half = n // 2
    tokens, width = normed.shape
    experts = n * xs
    chunk = rows.shape[-2]
    slots = sg_hbm.shape[1]
    e = lax.axis_index("expert")
    d = lax.axis_index("dp")
    hi, lo = lax.div(e, 2), lax.rem(e, 2)
    x, core = lax.div(d, 2), lax.rem(d, 2)

    def z_dev(k):
        return {"expert": lax.rem(hi + k, half) * 2 + lo, "dp": d}

    y_dev = {"expert": hi * 2 + 1 - lo, "dp": d}

    def x_dev(k):
        return {"expert": e, "dp": lax.rem(x + k, xs) * 2 + core}

    c_dev = {"expert": e, "dp": x * 2 + 1 - core}
    pending = []

    def send(src, dst, s_sem, r_sem, dev):
        copy = pltpu.make_async_remote_copy(
            src_ref=src, dst_ref=dst, send_sem=s_sem, recv_sem=r_sem,
            device_id=dev, device_id_type=MESH,
        )
        copy.start()
        pending.append(copy)

    def arrived(dst, s_sem, r_sem, dev):
        pltpu.make_async_remote_copy(
            src_ref=dst, dst_ref=dst, send_sem=s_sem, recv_sem=r_sem,
            device_id=dev, device_id_type=MESH,
        ).wait_recv()

    barrier = pltpu.get_barrier_semaphore()
    partners = [z_dev(k) for k in range(1, half)] + [y_dev]
    partners += [x_dev(k) for k in range(1, xs)] + [c_dev]
    for dev in partners:
        pl.semaphore_signal(barrier, inc=1, device_id=dev, device_id_type=MESH)

    loads = [
        pltpu.make_async_copy(a, b, load_sem.at[i])
        for i, (a, b) in enumerate(
            ((sg_hbm, sg), (su_hbm, su), (wg_hbm, wg), (wu_hbm, wu), (wd_hbm, wd))
        )
    ]
    for load in loads:
        load.start()

    expert_ids = lax.broadcasted_iota(jnp.int32, (experts, tokens), 0)
    tri = (
        lax.broadcasted_iota(jnp.int32, (tokens, tokens), 0)
        < lax.broadcasted_iota(jnp.int32, (tokens, tokens), 1)
    ).astype(F32).astype(BF16)
    for p, (routes, probs) in enumerate(((fr, fp), (br, bp))):
        hits = jnp.zeros((experts, tokens), F32)
        weight = jnp.zeros((experts, tokens), F32)
        for j in range(top):
            same = routes[j : j + 1, :] == expert_ids
            hits = hits + jnp.where(same, 1.0, 0.0)
            weight = weight + jnp.where(same, probs[j : j + 1, :], 0.0)
        before = jnp.dot(hits.astype(BF16), tri, preferred_element_type=F32)
        place = jnp.where(hits > 0.0, before, -1000000.0)
        for g in range(n):
            meta_s[g, 2 * p * xs : (2 * p + 1) * xs, :] = place[g * xs : (g + 1) * xs, :]
            meta_s[g, (2 * p + 1) * xs : (2 * p + 2) * xs, :] = weight[g * xs : (g + 1) * xs, :]
    meta_z[0, 0] = meta_s[e]
    sources = (normed, grad)
    for p in range(2):
        tok[p, 0, 0] = sources[p][...]

    pl.semaphore_wait(barrier, len(partners))

    send(meta_s.at[hi * 2 + 1 - lo], meta_y.at[0], my_sem.at[0, 0], my_sem.at[1, 0], y_dev)
    for k in range(1, half):
        to = lax.rem(hi + k, half) * 2
        for c in range(2):
            send(
                meta_s.at[to + (lo if c == 0 else 1 - lo)], meta_z.at[c, half - k],
                ms_sem.at[c, k], mr_sem.at[c, half - k], z_dev(k),
            )

    def start_y(p):
        send(sources[p], tok.at[p, 0, 1], ys_sem.at[p, 0], yr_sem.at[p, 0], y_dev)

    start_y(0)
    for p in range(2):
        for k in range(1, half):
            send(sources[p], tok.at[p, half - k, 0], zs_sem.at[p, k], zr_sem.at[p, half - k], z_dev(k))

    def forward_y(p, r):
        if r == 0:
            if p == 1:
                start_y(1)
            return
        if p == 0:
            for c in range(2):
                arrived(meta_z.at[c, r], ms_sem.at[c, r], mr_sem.at[c, r], z_dev(r))
            send(meta_z.at[1, r], meta_y.at[r], my_sem.at[0, r], my_sem.at[1, r], y_dev)
        arrived(tok.at[p, r, 0], zs_sem.at[p, r], zr_sem.at[p, r], z_dev(r))
        send(tok.at[p, r, 0], tok.at[p, r, 1], ys_sem.at[p, r], yr_sem.at[p, r], y_dev)

    def meta_row(c, r, row):
        if c == 0:
            return meta_z[0, r, pl.ds(row, 1), :]
        return meta_y[r, pl.ds(row, 1), :]

    def pack(p, r):
        if p == 0:
            arrived(meta_y.at[r], my_sem.at[0, r], my_sem.at[1, r], y_dev)
        arrived(tok.at[p, r, 1], ys_sem.at[p, r], yr_sem.at[p, r], y_dev)
        slot_ids = lax.broadcasted_iota(jnp.int32, (chunk, tokens), 0).astype(F32)
        block = tok[p, r].reshape(2 * tokens, width)
        for k in list(range(1, xs)) + [0]:
            line = 2 * p * xs + lax.rem(x + k, xs)
            parts = [
                jnp.where(slot_ids == meta_row(c, r, line) + float(c * cap), 1.0, 0.0).astype(BF16)
                for c in range(2)
            ]
            packed = jnp.dot(
                jnp.concatenate(parts, axis=1), block, preferred_element_type=F32
            ).astype(BF16)
            if k == 0:
                rows[p, r, 0, 0] = packed
                send(rows.at[p, r, 0, 0], rows.at[p, r, 0, 1], cs_sem.at[p, r, 0], cr_sem.at[p, r, 0], c_dev)
            else:
                stag[p, r, k] = packed
                send(stag.at[p, r, k], rows.at[p, r, xs - k, 0], xs_sem.at[p, r, k], xr_sem.at[p, r, xs - k], x_dev(k))

    def forward_core(p, r):
        for k in range(1, xs):
            arrived(rows.at[p, r, k, 0], xs_sem.at[p, r, k], xr_sem.at[p, r, k], x_dev(k))
            send(rows.at[p, r, k, 0], rows.at[p, r, k, 1], cs_sem.at[p, r, k], cr_sem.at[p, r, k], c_dev)

    def feature(k, other):
        at = lax.rem(x + k, xs) * 2 + (1 - core if other else core)
        return pl.ds(pl.multiple_of(at * width, width), width)

    nt = (((1,), (1,)), ((), ()))

    def compute(p, r):
        first, second = None, None
        for k in range(xs):
            for o in range(2):
                if o == 1:
                    arrived(rows.at[p, r, k, 1], cs_sem.at[p, r, k], cr_sem.at[p, r, k], c_dev)
                piece = rows[p, r, k, o]
                if p == 0:
                    a = lax.dot_general(piece, wg[:, feature(k, o)], nt, preferred_element_type=F32)
                    b = lax.dot_general(piece, wu[:, feature(k, o)], nt, preferred_element_type=F32)
                    first = a if first is None else first + a
                    second = b if second is None else second + b
                else:
                    a = lax.dot_general(piece, wd[:, feature(k, o)], nt, preferred_element_type=F32)
                    first = a if first is None else first + a
        if p == 0:
            hidden = (jax.nn.silu(first) * second).astype(BF16)
        else:
            grad_gate = (first * fac[0, r]).astype(BF16)
            grad_up = (first * fac[1, r]).astype(BF16)
        for o in (1, 0):
            for k in range(xs):
                if p == 0:
                    res = jnp.dot(hidden, wd[:, feature(k, o)], preferred_element_type=F32)
                else:
                    res = jnp.dot(grad_gate, wg[:, feature(k, o)], preferred_element_type=F32)
                    res = res + jnp.dot(grad_up, wu[:, feature(k, o)], preferred_element_type=F32)
                if o == 1:
                    half_s[p, r, k] = res.astype(BF16)
                    send(half_s.at[p, r, k], half_r.at[p, r, k], hs_sem.at[p, r, k], hr_sem.at[p, r, k], c_dev)
                else:
                    keep[p, r, k] = res.astype(BF16)

    def join(p, r):
        for k in list(range(1, xs)) + [0]:
            arrived(half_r.at[p, r, k], hs_sem.at[p, r, k], hr_sem.at[p, r, k], c_dev)
            total = (keep[p, r, k].astype(F32) + half_r[p, r, k].astype(F32)).astype(BF16)
            if k == 0:
                mixin[p, r, 0] = total
            else:
                eo_s[p, r, k] = total
                send(eo_s.at[p, r, k], mixin.at[p, r, xs - k], es_sem.at[p, r, k], er_sem.at[p, r, xs - k], x_dev(k))

    def mix(p, r):
        for k in range(1, xs):
            arrived(mixin.at[p, r, k], es_sem.at[p, r, k], er_sem.at[p, r, k], x_dev(k))
        slot_ids = lax.broadcasted_iota(jnp.int32, (tokens, chunk), 1).astype(F32)
        pad = round_up(2 * xs, 8) - 2 * xs
        for c in (1, 0):
            lines = []
            for k in range(xs):
                at = lax.rem(x + k, xs)
                lines.append(meta_row(c, r, 2 * p * xs + at))
                lines.append(meta_row(c, r, (2 * p + 1) * xs + at))
            if pad:
                lines.append(jnp.zeros((pad, tokens), F32))
            cols = jnp.concatenate(lines, axis=0).T
            out = jnp.zeros((tokens, width), F32)
            for k in range(xs):
                mat = jnp.where(
                    slot_ids == cols[:, 2 * k : 2 * k + 1] + float(c * cap),
                    cols[:, 2 * k + 1 : 2 * k + 2], 0.0,
                ).astype(BF16)
                out = out + jnp.dot(mat, mixin[p, r, k], preferred_element_type=F32)
            if c == 1:
                yout[p, r] = out.astype(BF16)
                send(yout.at[p, r], yin.at[p, r], ry_sem.at[0, p, r], ry_sem.at[1, p, r], y_dev)
            else:
                zacc[p, r] = out

    def scatter_z(p, r):
        arrived(yin.at[p, r], ry_sem.at[0, p, r], ry_sem.at[1, p, r], y_dev)
        total = zacc[p, r] + yin[p, r].astype(F32)
        if r == 0:
            zacc[p, 0] = total
        else:
            zout[p, r] = total.astype(BF16)
            send(zout.at[p, r], zin.at[p, half - r], rzs_sem.at[p, r], rzr_sem.at[p, half - r], z_dev(r))

    def finish(p):
        total = zacc[p, 0]
        for r in range(1, half):
            arrived(zin.at[p, r], rzs_sem.at[p, r], rzr_sem.at[p, r], z_dev(r))
            total = total + zin[p, r].astype(F32)
        (fwd_out, bwd_out)[p][...] = total

    def factors(r):
        at = lax.broadcasted_iota(jnp.int32, (chunk, slots), 0)
        late = at >= cap
        turn = hi + r
        turn = jnp.where(turn >= half, turn - half, turn)
        origin = jnp.where(late, (turn * 2 + 1 - lo) * cap - cap, (turn * 2 + lo) * cap) + at
        hit = (origin == lax.broadcasted_iota(jnp.int32, (chunk, slots), 1)) & (at < 2 * cap)
        perm = jnp.where(hit, 1.0, 0.0).astype(BF16)
        gval = lax.dot_general(perm, sg[...], nt, preferred_element_type=F32)
        uval = lax.dot_general(perm, su[...], nt, preferred_element_type=F32)
        sig = jax.nn.sigmoid(gval)
        fac[0, r] = uval * sig * (1.0 + gval * (1.0 - sig))
        fac[1, r] = gval * sig

    back = list(range(half - 1, 0, -1))
    items = [(0, 0), (1, 0)] + [(0, r) for r in back] + [(1, r) for r in back]
    count = len(items)
    stages = ((0, pack), (-1, forward_y), (1, forward_core), (1, compute), (2, mix), (1, join), (3, scatter_z))
    for load in loads[:2]:
        load.wait()
    for step in range(-2, count + 9):
        if step == 1:
            for load in loads[2:]:
                load.wait()
        for lag, stage in stages:
            if 0 <= step - lag < count:
                stage(*items[step - lag])
        if 0 <= step < half:
            factors(step)
    finish(0)
    finish(1)
    for copy in pending:
        copy.wait_send()


def body(
    fwd_resid, fwd_normed, fwd_routes, fwd_probs, bwd_grad, bwd_routes, bwd_probs,
    saved_gate, saved_up, w_gate, w_up, w_down,
):
    n = lax.axis_size("expert")
    dp = lax.axis_size("dp")
    sections = lax.axis_size("section")
    xs = dp // 2
    half = n // 2
    tokens, width = fwd_normed.shape[1:]
    top = fwd_routes.shape[2]
    slots, hidden = saved_gate.shape[2:]
    feats = w_gate.shape[2]
    cap = slots // n
    chunk = round_up(2 * cap, 8)
    meta_rows = 4 * xs
    vmem = pl.BlockSpec(memory_space=pltpu.VMEM)
    hbm = pl.BlockSpec(memory_space=pl.ANY)
    dma = pltpu.SemaphoreType.DMA
    out = jax.ShapeDtypeStruct((tokens, width), F32)
    fwd_sum, bwd_sum = pl.pallas_call(
        functools.partial(kernel, n, xs, top, cap),
        out_shape=(out, out),
        in_specs=[vmem] * 6 + [hbm] * 5,
        out_specs=(vmem, vmem),
        scratch_shapes=[
            pltpu.VMEM((hidden, slots), BF16),
            pltpu.VMEM((hidden, slots), BF16),
            pltpu.VMEM((hidden, feats), BF16),
            pltpu.VMEM((hidden, feats), BF16),
            pltpu.VMEM((hidden, feats), BF16),
            pltpu.VMEM((2, half, chunk, hidden), F32),
            pltpu.VMEM((n, meta_rows, tokens), F32),
            pltpu.VMEM((2, half, meta_rows, tokens), F32),
            pltpu.VMEM((half, meta_rows, tokens), F32),
            pltpu.VMEM((2, half, 2, tokens, width), BF16),
            pltpu.VMEM((2, half, xs, 2, chunk, width), BF16),
            pltpu.VMEM((2, half, xs, chunk, width), BF16),
            pltpu.VMEM((2, half, xs, chunk, width), BF16),
            pltpu.VMEM((2, half, xs, chunk, width), BF16),
            pltpu.VMEM((2, half, xs, chunk, width), BF16),
            pltpu.VMEM((2, half, xs, chunk, width), BF16),
            pltpu.VMEM((2, half, xs, chunk, width), BF16),
            pltpu.VMEM((2, half, tokens, width), BF16),
            pltpu.VMEM((2, half, tokens, width), BF16),
            pltpu.VMEM((2, half, tokens, width), F32),
            pltpu.VMEM((2, half, tokens, width), BF16),
            pltpu.VMEM((2, half, tokens, width), BF16),
            dma((5,)),
            dma((2, half)), dma((2, half)), dma((2, half)),
            dma((2, half)), dma((2, half)), dma((2, half)), dma((2, half)),
            dma((2, half, xs)), dma((2, half, xs)), dma((2, half, xs)), dma((2, half, xs)),
            dma((2, half, xs)), dma((2, half, xs)), dma((2, half, xs)), dma((2, half, xs)),
            dma((2, 2, half)), dma((2, half)), dma((2, half)),
        ],
        compiler_params=pltpu.CompilerParams(
            collective_id=0, has_side_effects=True, vmem_limit_bytes=60 * 1024 * 1024
        ),
    )(
        fwd_normed[0], bwd_grad[0],
        fwd_routes[0].T, fwd_probs[0].T, bwd_routes[0].T, bwd_probs[0].T,
        saved_gate[0, 0].T, saved_up[0, 0].T, w_gate[0, 0].T, w_up[0, 0].T, w_down[0, 0],
    )
    fwd_next = (fwd_resid.astype(F32) + fwd_sum[None]).astype(BF16)
    bwd_next = bwd_sum[None].astype(BF16)
    if sections > 1:
        up = [(i, (i + 1) % sections) for i in range(sections)]
        fwd_next = lax.ppermute(fwd_next, "section", up)
        bwd_next = lax.ppermute(bwd_next, "section", [(j, i) for i, j in up])
    return (fwd_next, bwd_next)


def solution(mesh):
    tok = P("section", "expert", "dp")
    route = P("section", "expert", None)
    unit = P("section", ("expert", "dp"), None, None)
    return jax.shard_map(
        body,
        mesh=mesh,
        in_specs=(tok, tok, route, route, tok, route, route, unit, unit, unit, unit, unit),
        out_specs=(tok, tok),
        check_vma=False,
    )
```
